32 devices in a mesh: gx: 16 (over z, y, core), gy: 2 (over x).
Axes of the slice: x: 2, y: 2, z: 4, core: 2. Of those that a mesh axis runs over, the one named last changes fastest.
Arguments:
- populations: float32 [19, 128, 32, 128], P(None, 'gx', 'gy'), may hold values from 0.5 to 2
- ion_density: float32 [2, 128, 32, 128], P(None, 'gx', 'gy'), may hold values from 0.5 to 1.5
- potential: float32 [128, 32, 128], P('gx', 'gy'), may hold values from -6 to 6
- node_flags: int32 [128, 32, 128], P('gx', 'gy'), may hold values from 0 to 64, as said below
- colloid_count: int32 [16, 2], P('gx', 'gy'), may hold values from 0 to 2, as said below
- colloid_centre: int32 [3, 16, 2, 2], P(None, 'gx', 'gy'), may hold values from 0 to 127, as said below
- colloid_velocity: float32 [3, 16, 2, 2], P(None, 'gx', 'gy'), may hold values from -0.5 to 0.5
- colloid_spin: float32 [3, 16, 2, 2], P(None, 'gx', 'gy'), may hold values from -0.1 to 0.1
- bead_cell: int32 [16, 2, 2, 2562], P('gx', 'gy'), may hold values from 0 to 2196
- bead_frac: float32 [3, 16, 2, 2, 2562], P(None, 'gx', 'gy'), may hold values from 0 to 1
- bead_weight: float32 [16, 2, 2, 2562], P('gx', 'gy'), may hold values from 0.25 to 1
Outputs:
- populations_next: float32 [19, 128, 32, 128], P(None, 'gx', 'gy')
- ion_density_next: float32 [2, 128, 32, 128], P(None, 'gx', 'gy')
- potential_next: float32 [128, 32, 128], P('gx', 'gy')
- colloid_kick: float32 [6, 16, 2, 2], P(None, 'gx', 'gy')
The draws below stay inside these ranges and needn't reach their ends.
Inputs may be any that keep to these rules, and one draw needn't show every extreme that they name: `node_flags`: bits 0 to 5 of a node's flag are 1 where the faces toward -x, +x, -y, +y, -z, +z are open, that is where the node and the neighbour across the face (periodic along all axes) are both fluid; bit 6 marks solid nodes; the nodes at z = 0 and z = 127 are solid; bit 1 of a node equals bit 0 of the next node along x, bit 3 equals bit 2 of the next node along y, bit 5 equals bit 4 of the next node along z. `colloid_count`: slots 0 to count - 1 of a brick hold colloids, the others are to be ignored; some brick has 2. `colloid_centre`: the centre of slot s of brick (i, j) lies in that brick: x in [i * 8, (i + 1) * 8), y in [j * 16, (j + 1) * 16), z in [7, 120].
All inputs are finite; a program needn't handle non-finite values.
Results may differ from the reference program's by a relative error of at most 0.0001.
Values sent between devices are 32-bit elements; how exact they have to be, the bound alone decides.
A program may use at most 128 MiB of HBM per device.

```python
import math
import jax
import jax.numpy as jnp
import numpy as np

CX = 8
CY = 16
NZ = 128
CSLOT = 2
BEADS = 2562
RADIUS = 6
SWEEPS = 2
BX = 16
BY = 2
NX = 128
NY = 32


def draw_node_flags(key, part):
    solid = jax.random.randint(key, (NX, NY, NZ), 0, 12) == 0
    depth_index = jnp.arange(NZ)
    walls = (depth_index == 0) | (depth_index == NZ - 1)
    fluid = jnp.where(solid | walls[None, None, :], 0, 1).astype(jnp.int32)
    total_flags = fluid * jnp.roll(fluid, 1, 0)
    total_flags = total_flags + 2 * fluid * jnp.roll(fluid, -1, 0)
    total_flags = total_flags + 4 * fluid * jnp.roll(fluid, 1, 1)
    total_flags = total_flags + 8 * fluid * jnp.roll(fluid, -1, 1)
    total_flags = total_flags + 16 * fluid * jnp.roll(fluid, 1, 2)
    total_flags = total_flags + 32 * fluid * jnp.roll(fluid, -1, 2)
    return (total_flags + 64 * (1 - fluid)).astype(jnp.int32)


def draw_colloid_count(key, part):
    first_key, second_key = jax.random.split(key)
    counts = jax.random.randint(first_key, (BX * BY,), 0, CSLOT + 1)
    chosen = jax.random.randint(second_key, (), 0, BX * BY)
    counts = jnp.where(jnp.arange(BX * BY) == chosen, CSLOT, counts)
    return counts.reshape(BX, BY).astype(jnp.int32)


def draw_colloid_centre(key, part):
    keys_all = jax.random.split(key, 3)
    local_x = jax.random.randint(keys_all[0], (BX, BY, CSLOT), 0, CX)
    local_y = jax.random.randint(keys_all[1], (BX, BY, CSLOT), 0, CY)
    depth_pick = jax.random.randint(keys_all[2], (BX, BY, CSLOT), RADIUS + 1, NZ - RADIUS - 1)
    anchor_x = jnp.arange(BX)[:, None, None] * CX
    anchor_y = jnp.arange(BY)[None, :, None] * CY
    return jnp.stack([local_x + anchor_x, local_y + anchor_y, depth_pick]).astype(jnp.int32)


def touch_ends(entries, own_key, least, top_value):
    place = [jax.random.randint(jax.random.fold_in(own_key, axis), (), 0, length) for axis, length in enumerate(entries.shape)]
    longest = entries.shape.index(max(entries.shape))
    beside = place[:longest] + [(place[longest] + 1) % entries.shape[longest]] + place[longest + 1:]
    return entries.at[tuple(place)].set(least).at[tuple(beside)].set(top_value)


def shard_levels(key, shape, shards, low, top_value):
    def one(dim, parts):
        draws = jax.random.uniform(jax.random.fold_in(jax.random.fold_in(key, 6), dim), (parts,), jnp.float32, low / len(shards), top_value / len(shards))
        return jnp.repeat(jnp.exp(draws), shape[dim] // parts).reshape((-1,) + (1,) * (len(shape) - dim - 1))

    gain = one(*shards[0])
    for cut in shards[1:]:
        gain = gain * one(*cut)
    return gain


def noise(key, dims, scale, reach, shards=(), dtype=jnp.bfloat16):
    values = jax.random.normal(key, dims, jnp.float32) * scale
    if len(shards) > 0:
        values = shard_levels(key, dims, shards, -0.22, 0.18) * values
    return jnp.clip(values, min=-reach, max=reach).astype(dtype)


def setup_inputs(seed: int = 0) -> dict:
    keys = jax.random.split(jax.random.key(seed), 12)
    return {
        "populations": jnp.clip(0.5 + 1.5 * jax.random.uniform(keys[0], (19, NX, NY, NZ), jnp.float32) ** shard_levels(keys[0], (19, NX, NY, NZ), ((1, 16), (2, 2)), -0.2, 0.2), 0.5, 2.0),
        "ion_density": jnp.clip(0.5 + 1.0 * jax.random.uniform(keys[1], (2, NX, NY, NZ), jnp.float32) ** shard_levels(keys[1], (2, NX, NY, NZ), ((1, 16), (2, 2)), -0.2, 0.2), 0.5, 1.5),
        "potential": noise(keys[2], (NX, NY, NZ), 1.0, 6.0, ((0, 16), (1, 2)), jnp.float32),
        "node_flags": draw_node_flags(jax.random.fold_in(keys[11], 71), 0),
        "colloid_count": draw_colloid_count(jax.random.fold_in(keys[11], 71), 0),
        "colloid_centre": draw_colloid_centre(jax.random.fold_in(keys[11], 71), 0),
        "colloid_velocity": noise(keys[6], (3, BX, BY, CSLOT), 0.1, 0.5, ((1, 16), (2, 2)), jnp.float32),
        "colloid_spin": noise(keys[7], (3, BX, BY, CSLOT), 0.02, 0.1, ((1, 16), (2, 2)), jnp.float32),
        "bead_cell": touch_ends(jax.random.randint(keys[8], (BX, BY, CSLOT, BEADS), 0, (2 * RADIUS + 1) * (2 * RADIUS + 1) * (2 * RADIUS + 1)), jax.random.fold_in(keys[8], 1), 0, ((2 * RADIUS + 1) * (2 * RADIUS + 1) * (2 * RADIUS + 1)) - 1).astype(jnp.int32),
        "bead_frac": jnp.clip(1.0 * jax.random.uniform(keys[9], (3, BX, BY, CSLOT, BEADS), jnp.float32) ** shard_levels(keys[9], (3, BX, BY, CSLOT, BEADS), ((1, 16), (2, 2)), -0.2, 0.2), 0.0, 1.0),
        "bead_weight": jnp.clip(jnp.exp(math.log(1.0) - 1.3862944 * jax.random.uniform(keys[10], (BX, BY, CSLOT, BEADS), jnp.float32) ** shard_levels(keys[10], (BX, BY, CSLOT, BEADS), ((0, 16), (1, 2)), -0.2, 0.2)), 0.25, 1.0),
    }


LATTICE = np.array([[0, 0, 0], [1, 0, 0], [-1, 0, 0], [0, 1, 0], [0, -1, 0], [0, 0, 1], [0, 0, -1],
                    [1, 1, 0], [-1, -1, 0], [1, -1, 0], [-1, 1, 0], [1, 0, 1], [-1, 0, -1], [1, 0, -1],
                    [-1, 0, 1], [0, 1, 1], [0, -1, -1], [0, 1, -1], [0, -1, 1]])
OPPOSITE = np.array([0, 2, 1, 4, 3, 6, 5, 8, 7, 10, 9, 12, 11, 14, 13, 16, 15, 18, 17])
PLUS_SETS = [np.array([i for i in range(19) if LATTICE[i][a] == 1]) for a in range(3)]
MINUS_SETS = [np.array([i for i in range(19) if LATTICE[i][a] == -1]) for a in range(3)]
tau_relax = 0.8
kappa_charge = 0.5
friction = 4.0
diffusion = (0.12, 0.15)
valence = (1.0, -1.0)


def lattice_weight(i):
    if i == 0:
        return 1.0 / 3.0
    if i < 7:
        return 1.0 / 18.0
    return 1.0 / 36.0


def flag_bit(node_flags, bit):
    return ((node_flags // (2 ** bit)) % 2).astype(jnp.float32)


def moments(pops):
    rows_out = []
    for a in range(3):
        rows_out.append(jnp.sum(pops[PLUS_SETS[a]], 0) - jnp.sum(pops[MINUS_SETS[a]], 0))
    return jnp.stack(rows_out)


def cross_product(left, right):
    return jnp.stack([left[1] * right[2] - left[2] * right[1],
                      left[2] * right[0] - left[0] * right[2],
                      left[0] * right[1] - left[1] * right[0]])


def face_flux(low_ion, high_ion, low_phi, high_phi, low_drift, high_drift, open_face, s):
    middle = 0.5 * (low_ion + high_ion)
    diffusive = -diffusion[s] * ((high_ion - low_ion) + valence[s] * middle * (high_phi - low_phi))
    return open_face * (diffusive + 0.5 * (low_drift + high_drift) * middle)


def collide(read, density, velocity, force, solid):
    shifted = velocity + tau_relax * force / density
    speed_sq = shifted[0] * shifted[0] + shifted[1] * shifted[1] + shifted[2] * shifted[2]
    results = []
    for i in range(19):
        along_link = jnp.zeros_like(density)
        for a in range(3):
            if LATTICE[i][a] != 0:
                along_link = along_link + float(LATTICE[i][a]) * shifted[a]
        equilibrium = lattice_weight(i) * density * (1.0 + 3.0 * along_link + 4.5 * along_link * along_link - 1.5 * speed_sq)
        results.append(read[i] - (read[i] - equilibrium) / tau_relax)
    relaxed = jnp.stack(results)
    return jnp.where(solid[None] > 0.5, read[OPPOSITE], relaxed)


def neighbour_sum(field):
    z_padded = jnp.pad(field, ((0, 0), (0, 0), (1, 1)))
    return (jnp.roll(field, -1, 0) + jnp.roll(field, 1, 0) + jnp.roll(field, -1, 1) + jnp.roll(field, 1, 1)
            + z_padded[:, :, 2:] + z_padded[:, :, :-2])


def electric_field(field):
    z_padded = jnp.pad(field, ((0, 0), (0, 0), (1, 1)))
    return jnp.stack([-(jnp.roll(field, -1, 0) - jnp.roll(field, 1, 0)) / 2.0,
                      -(jnp.roll(field, -1, 1) - jnp.roll(field, 1, 1)) / 2.0,
                      -(z_padded[:, :, 2:] - z_padded[:, :, :-2]) / 2.0])


def reference(populations, ion_density, potential, node_flags, colloid_count, colloid_centre,
              colloid_velocity, colloid_spin, bead_cell, bead_frac, bead_weight):
    density_old = jnp.sum(populations, 0)
    drift = moments(populations) / density_old
    charge = ion_density[0] - ion_density[1]
    potential_now = potential
    for sweep_step in range(SWEEPS):
        potential_now = (neighbour_sum(potential_now) + kappa_charge * charge) / 6.0
    new_ions = []
    for s in range(2):
        ions = ion_density[s]
        divergence = jnp.zeros_like(ions)
        for a in range(3):
            fluxes = face_flux(jnp.roll(ions, 1, a), ions, jnp.roll(potential_now, 1, a), potential_now,
                               jnp.roll(drift[a], 1, a), drift[a], flag_bit(node_flags, 2 * a), s)
            divergence = divergence + (jnp.roll(fluxes, -1, a) - fluxes)
        new_ions.append(ions - divergence)
    read = jnp.stack([jnp.roll(populations[i], (int(LATTICE[i][0]), int(LATTICE[i][1]), int(LATTICE[i][2])), (0, 1, 2))
                          for i in range(19)])
    density = jnp.sum(read, 0)
    velocity = moments(read) / density
    cube_side = 2 * RADIUS + 1
    step_x = bead_cell // (cube_side * cube_side) - RADIUS
    step_y = (bead_cell // cube_side) % cube_side - RADIUS
    step_z = bead_cell % cube_side - RADIUS
    lever = jnp.stack([step_x.astype(jnp.float32) + bead_frac[0], step_y.astype(jnp.float32) + bead_frac[1],
                       step_z.astype(jnp.float32) + bead_frac[2]])
    bead_velocity = colloid_velocity[..., None] + cross_product(colloid_spin[..., None], lever)
    filled = (jnp.arange(CSLOT)[None, None, :] < colloid_count[:, :, None]).astype(jnp.float32)
    weight = bead_weight * filled[..., None]
    node_x = (colloid_centre[0][..., None] + step_x) % NX
    node_y = (colloid_centre[1][..., None] + step_y) % NY
    node_z = colloid_centre[2][..., None] + step_z
    node_index = ((node_x * NY + node_y) * NZ + node_z).astype(jnp.int32)
    sampled = velocity.reshape(3, -1)[:, node_index]
    bead_force = friction * weight * (bead_velocity - sampled)
    node_force = jnp.zeros((3, NX * NY * NZ), jnp.float32).at[:, node_index.reshape(-1)].add(bead_force.reshape(3, -1))
    node_force = node_force.reshape(3, NX, NY, NZ)
    torque = cross_product(lever, bead_force)
    colloid_kick = -jnp.concatenate([jnp.sum(bead_force, -1), jnp.sum(torque, -1)], 0) / BEADS
    force = charge[None] * electric_field(potential_now) + node_force
    populations_next = collide(read, density, velocity, force, flag_bit(node_flags, 6))
    return populations_next, jnp.stack(new_ions), potential_now, colloid_kick
```

```python
import functools

import jax
import jax.numpy as jnp
import numpy as np
from jax import lax
from jax.experimental import pallas as pl
from jax.experimental.pallas import tpu as pltpu
from jax.sharding import PartitionSpec as P

RADIUS = 6
SIDE = 2 * RADIUS + 1
YO = 8
XO = 3
CHUNK = 384
MESH = pl.DeviceIdType.MESH
F32 = jnp.float32
BF16 = jnp.bfloat16

LATTICE = np.array(
    [
        [0, 0, 0],
        [1, 0, 0],
        [-1, 0, 0],
        [0, 1, 0],
        [0, -1, 0],
        [0, 0, 1],
        [0, 0, -1],
        [1, 1, 0],
        [-1, -1, 0],
        [1, -1, 0],
        [-1, 1, 0],
        [1, 0, 1],
        [-1, 0, -1],
        [1, 0, -1],
        [-1, 0, 1],
        [0, 1, 1],
        [0, -1, -1],
        [0, 1, -1],
        [0, -1, 1],
    ]
)
OPPOSITE = [0, 2, 1, 4, 3, 6, 5, 8, 7, 10, 9, 12, 11, 14, 13, 16, 15, 18, 17]
tau_relax = 0.8
kappa_charge = 0.5
friction = 4.0
diffusion = (0.12, 0.15)
valence = (1.0, -1.0)
X_DIRS = [(1, 0), (-1, 0)]
Y_DIRS = [(0, 1), (0, -1)]
C_DIRS = [(1, 1), (1, -1), (-1, 1), (-1, -1)]
DIRS = X_DIRS + Y_DIRS + C_DIRS


def lattice_weight(i):
    if i == 0:
        return 1.0 / 3.0
    if i < 7:
        return 1.0 / 18.0
    return 1.0 / 36.0


def links(a, sign):
    return [i for i in range(19) if LATTICE[i][a] == sign]


def corner_link(sx, sy):
    return [i for i in range(19) if tuple(LATTICE[i]) == (sx, sy, 0)][0]


def total_of(terms):
    terms = list(terms)
    while len(terms) > 1:
        terms = [
            terms[j] + terms[j + 1] if j + 1 < len(terms) else terms[j]
            for j in range(0, len(terms), 2)
        ]
    return terms[0]


def momentum(pops, a):
    return total_of(pops[i] for i in links(a, 1)) - total_of(pops[i] for i in links(a, -1))


def layer(s, depth, width):
    return width - 1 - depth if s > 0 else depth


def halo(s, depth, width):
    return -1 - depth if s > 0 else width + depth


def split3(v):
    hi = v.astype(BF16)
    rest = v - hi.astype(F32)
    mid = rest.astype(BF16)
    low = (rest - mid.astype(F32)).astype(BF16)
    return hi, mid, low


def dot_t(a, b):
    return lax.dot_general(a, b, (((1,), (1,)), ((), ())), preferred_element_type=F32)


def bead_span_x(sx, width):
    if sx > 0:
        return RADIUS + width, RADIUS, 0
    if sx < 0:
        return 0, RADIUS, width - RADIUS
    return RADIUS, width, 0


def bead_span_y(sy, width):
    if sy > 0:
        return YO + width, 8, 0
    if sy < 0:
        return 0, 8, width - 8
    return YO, width, 0


def pack_kernel(
    count_ref, centre_ref, vel_ref, spin_ref, cell_ref, frac_ref, weight_ref, pops_ref, ions_ref,
    phi_ref, xs_ref, ys_ref, cs_ref, own_ref, drift_ref, base_ref,
    beads, codes, acc, field,
):
    wx, wy, depth = phi_ref.shape
    nb = cell_ref.shape[3]
    kp = beads.shape[2]
    tall = 2 * YO + wy
    planes = wx + 2 * RADIUS

    def drift_plane(x, carry):
        pops = [pops_ref[i, x] for i in range(19)]
        inv = 1.0 / total_of(pops)
        for a in range(3):
            drift_ref[a, x] = momentum(pops, a) * inv
        return carry

    lax.fori_loop(0, wx, drift_plane, 0)

    beads[...] = jnp.zeros_like(beads)
    beads[0, :, :nb] = cell_ref[0, 0].astype(F32)
    for k in range(3):
        beads[1 + k, :, :nb] = frac_ref[k, 0, 0]
    beads[4, :, :nb] = weight_ref[0, 0]
    first = lax.broadcasted_iota(jnp.int32, (2, kp), 0) == 0
    count = count_ref[0, 0]

    def pick(ref, k):
        return jnp.where(first, ref[k, 0, 0, 0], ref[k, 0, 0, 1])

    cell = beads[0]
    ix = jnp.floor((cell + 0.5) * (1.0 / (SIDE * SIDE)))
    rest = cell - ix * (SIDE * SIDE)
    iy = jnp.floor((rest + 0.5) * (1.0 / SIDE))
    iz = rest - iy * SIDE
    slot = jnp.where(first, 0, 1)
    weight = jnp.where(slot < count, beads[4], 0.0)
    lever = [idx - RADIUS + beads[1 + k] for k, idx in enumerate((ix, iy, iz))]
    vel = [pick(vel_ref, k) for k in range(3)]
    spin = [pick(spin_ref, k) for k in range(3)]
    cross = lambda p, q: [p[1] * q[2] - p[2] * q[1], p[2] * q[0] - p[0] * q[2], p[0] * q[1] - p[1] * q[0]]
    turn = cross(spin, lever)
    push = [weight * (vel[k] + turn[k]) for k in range(3)]
    twist = cross(lever, push)
    for k, v in enumerate(push + twist):
        base_ref[k] = jnp.broadcast_to(jnp.sum(v, axis=1, keepdims=True), (2, 128))
    local_x = [lax.rem(centre_ref[0, 0, 0, s], wx).astype(F32) for s in range(2)]
    local_y = [lax.rem(centre_ref[1, 0, 0, s], wy).astype(F32) for s in range(2)]
    px = ix + jnp.where(first, local_x[0], local_x[1])
    py = iy + jnp.where(first, local_y[0], local_y[1]) + (YO - RADIUS)
    codes[0] = px * tall + py
    codes[1] = iz
    codes[2] = weight
    for k in range(3):
        codes[3 + k] = weight * lever[k]
    for s in range(2):
        acc[...] = jnp.zeros_like(acc)

        def step(c, carry):
            lanes = pl.ds(pl.multiple_of(c * CHUNK, CHUNK), CHUNK)
            code = codes[0, s : s + 1, lanes].astype(jnp.int32)
            node = lax.broadcasted_iota(jnp.int32, (planes * tall, CHUNK), 0)
            place = jnp.where(node == code, 1.0, 0.0).astype(BF16)
            level = codes[1, s : s + 1, lanes].astype(jnp.int32)
            at_level = lax.broadcasted_iota(jnp.int32, (16, CHUNK), 0) == level
            values = jnp.concatenate(
                [jnp.where(at_level, codes[2 + q, s : s + 1, lanes], 0.0) for q in range(4)], 0
            )
            parts = jnp.concatenate(split3(values), 0)
            acc[...] += dot_t(place, parts)
            return carry

        lax.fori_loop(0, kp // CHUNK, step, 0)
        field[:, 64 * s : 64 * s + 64] = acc[:, 0:64] + acc[:, 64:128] + acc[:, 128:192]

    lane = lax.broadcasted_iota(jnp.int32, (1, 128), 1)
    lane_slot = lane // 64
    channel = (lane // 16) % 4
    by_slot = lambda ref, k: jnp.where(lane_slot == 0, ref[k, 0, 0, 0], ref[k, 0, 0, 1])
    v = [by_slot(vel_ref, k) for k in range(3)]
    w = [by_slot(spin_ref, k) for k in range(3)]
    zero = jnp.zeros((1, 128), F32)

    def four(*rows):
        out = zero
        for q, row in enumerate(rows):
            out = jnp.where(channel == q, row, out)
        return out

    constants = jnp.concatenate(
        [
            four(v[0], zero, -w[2], w[1]),
            four(v[1], w[2], zero, -w[0]),
            four(v[2], -w[1], w[0], zero),
            four(zero + 1.0, zero, zero, zero),
            by_slot(centre_ref, 2).astype(F32) + (lane % 16 - RADIUS).astype(F32),
            zero,
            zero,
            zero,
        ],
        0,
    )

    def charge(x, y):
        return ions_ref[0, x, y] - ions_ref[1, x, y]

    def put_beads(ref, at, sx, sy):
        x0, nx, _ = bead_span_x(sx, wx)
        y0, ny, _ = bead_span_y(sy, wy)
        for x in range(nx):
            start = (x0 + x) * tall + y0
            ref[pl.ds(at + x * ny, ny)] = field[start : start + ny]
        return at + nx * ny

    own_ref[0:8] = constants
    put_beads(own_ref, 8, 0, 0)
    for j, (sx, _) in enumerate(X_DIRS):
        out = xs_ref.at[j]
        out[0:8] = constants
        at = put_beads(out, 8, sx, 0)
        edge = layer(sx, 0, wx)
        rows = [pops_ref[i, edge] for i in links(0, sx)]
        rows += [ions_ref[0, edge], ions_ref[1, edge], charge(layer(sx, 1, wx), slice(None))]
        rows += [phi_ref[layer(sx, l, wx)] for l in range(3)] + [drift_ref[0, edge]]
        for row in rows:
            out[at : at + wy] = row
            at += wy
    for j, (_, sy) in enumerate(Y_DIRS):
        out = ys_ref.at[j]
        out[0:8] = constants
        at = put_beads(out, 8, 0, sy)
        edge = layer(sy, 0, wy)
        rows = [pops_ref[i, :, edge] for i in links(1, sy)]
        rows += [ions_ref[0, :, edge], ions_ref[1, :, edge], charge(slice(None), layer(sy, 1, wy))]
        rows += [phi_ref[:, layer(sy, l, wy)] for l in range(3)] + [drift_ref[1, :, edge]]
        for row in rows:
            out[at : at + wx] = row
            at += wx
    for j, (sx, sy) in enumerate(C_DIRS):
        out = cs_ref.at[j]
        out[0:8] = constants
        at = put_beads(out, 8, sx, sy)
        ex, ey = layer(sx, 0, wx), layer(sy, 0, wy)
        rows = [
            pops_ref[corner_link(sx, sy), ex, ey],
            charge(ex, ey),
            phi_ref[ex, ey],
            phi_ref[layer(sx, 1, wx), ey],
            phi_ref[ex, layer(sy, 1, wy)],
        ]
        for row in rows:
            out[at] = row
            at += 1
        out[at : at + 3] = jnp.zeros((3, 128), F32)


def neighbour(shape, sx, sy):
    nx, ny = shape
    return (
        lax.rem(lax.axis_index("gx") + (sx + nx), nx),
        lax.rem(lax.axis_index("gy") + (sy + ny), ny),
    )


def meet(shape):
    barrier = pltpu.get_barrier_semaphore()
    for sx, sy in DIRS:
        pl.semaphore_signal(barrier, inc=1, device_id=neighbour(shape, sx, sy), device_id_type=MESH)
    pl.semaphore_wait(barrier, len(DIRS))


def exchange_kernel(shape, xs, ys, cs, rx, ry, rc, send, recv):
    meet(shape)
    copies = []
    sources = [xs.at[0], xs.at[1], ys.at[0], ys.at[1]] + [cs.at[j] for j in range(4)]
    targets = [rx.at[0], rx.at[1], ry.at[0], ry.at[1]] + [rc.at[j] for j in range(4)]
    for d in range(8):
        copies.append(
            pltpu.make_async_remote_copy(
                src_ref=sources[d], dst_ref=targets[d], send_sem=send.at[d], recv_sem=recv.at[d],
                device_id=neighbour(shape, *DIRS[d]), device_id_type=MESH,
            )
        )
    for copy in copies:
        copy.start()
    for copy in copies:
        copy.wait()


def return_kernel(shape, beads, part_ref, base_ref, kick_ref, got, send, recv):
    meet(shape)
    copies = []
    for d, (sx, sy) in enumerate(DIRS):
        copies.append(
            pltpu.make_async_remote_copy(
                src_ref=part_ref.at[d + 1], dst_ref=got.at[d], send_sem=send.at[d],
                recv_sem=recv.at[d], device_id=neighbour(shape, -sx, -sy), device_id_type=MESH,
            )
        )
    for copy in copies:
        copy.start()
    for copy in copies:
        copy.wait()
    whole = total_of([part_ref[0]] + [got[d] for d in range(8)])
    lane = lax.broadcasted_iota(jnp.int32, (8, 128), 1)
    group = lane // 16
    for s in range(2):
        m = [
            jnp.sum(jnp.where(group == 4 * s + q, whole, 0.0), axis=1, keepdims=True)
            for q in range(4)
        ]
        mean = [m[0][k : k + 1] for k in range(3)]
        lev = [[m[1 + a][k : k + 1] for k in range(3)] for a in range(3)]
        turned = [lev[1][2] - lev[2][1], lev[2][0] - lev[0][2], lev[0][1] - lev[1][0]]
        for k, v in enumerate(mean + turned):
            value = (base_ref[k, s : s + 1] - v) * (-friction / beads)
            kick_ref[k, s : s + 1] = value


def main_kernel(
    pops_ref, ions_ref, phi_ref, flags_ref, drift_ref, own_ref, rx, ry, rc,
    pops_out, ions_out, phi_out, part_ref,
    ext, eion, echarge, edrift, ephi, ephi1, ephi2, held, marks, bead_rows, pushes, vels,
):
    wx, wy, depth = phi_ref.shape
    inner = slice(YO, YO + wy)
    lanes = lax.broadcasted_iota(jnp.int32, (1, depth), 1)

    for i in range(19):
        ext[i, 1 : 1 + wx, inner] = pops_ref[i]
    for s in range(2):
        eion[s, 1 : 1 + wx, inner] = ions_ref[s]
    echarge[XO : XO + wx, inner] = ions_ref[0] - ions_ref[1]
    ephi[XO : XO + wx, inner] = phi_ref[...]
    for a in range(2):
        edrift[a, 1 : 1 + wx, inner] = drift_ref[a]
    held[...] = jnp.zeros_like(held)

    def take_beads(ref, n, sx, sy):
        _, nx, tx = bead_span_x(sx, wx)
        _, ny, ty = bead_span_y(sy, wy)
        marks[n] = ref[0:8]
        for x in range(nx):
            held[n, tx + x, ty : ty + ny] = ref[8 + x * ny : 8 + (x + 1) * ny]
        return 8 + nx * ny

    take_beads(own_ref, 0, 0, 0)
    for j, (sx, _) in enumerate(X_DIRS):
        src = rx.at[j]
        at = take_beads(src, 1 + j, sx, 0)
        edge = 1 + halo(sx, 0, wx)
        for i in links(0, sx):
            ext[i, edge, inner] = src[at : at + wy]
            at += wy
        for s in range(2):
            eion[s, edge, inner] = src[at : at + wy]
            at += wy
        echarge[XO + halo(sx, 0, wx), inner] = eion[0, edge, inner] - eion[1, edge, inner]
        echarge[XO + halo(sx, 1, wx), inner] = src[at : at + wy]
        at += wy
        for l in range(3):
            ephi[XO + halo(sx, l, wx), inner] = src[at : at + wy]
            at += wy
        edrift[0, edge, inner] = src[at : at + wy]
    for j, (_, sy) in enumerate(Y_DIRS):
        src = ry.at[j]
        at = take_beads(src, 3 + j, 0, sy)
        edge = YO + halo(sy, 0, wy)
        for i in links(1, sy):
            ext[i, 1 : 1 + wx, edge] = src[at : at + wx]
            at += wx
        ion0, ion1 = src[at : at + wx], src[at + wx : at + 2 * wx]
        eion[0, 1 : 1 + wx, edge] = ion0
        eion[1, 1 : 1 + wx, edge] = ion1
        at += 2 * wx
        echarge[XO : XO + wx, edge] = ion0 - ion1
        echarge[XO : XO + wx, YO + halo(sy, 1, wy)] = src[at : at + wx]
        at += wx
        for l in range(3):
            ephi[XO : XO + wx, YO + halo(sy, l, wy)] = src[at : at + wx]
            at += wx
        edrift[1, 1 : 1 + wx, edge] = src[at : at + wx]
    for j, (sx, sy) in enumerate(C_DIRS):
        src = rc.at[j]
        at = take_beads(src, 5 + j, sx, sy)
        hx, hy = halo(sx, 0, wx), YO + halo(sy, 0, wy)
        ext[corner_link(sx, sy), 1 + hx, hy] = src[at]
        echarge[XO + hx, hy] = src[at + 1]
        ephi[XO + hx, hy] = src[at + 2]
        ephi[XO + halo(sx, 1, wx), hy] = src[at + 3]
        ephi[XO + hx, YO + halo(sy, 1, wy)] = src[at + 4]

    def up(v):
        return jnp.where(lanes == depth - 1, 0.0, pltpu.roll(v, depth - 1, v.ndim - 1))

    def down(v):
        return jnp.where(lanes == 0, 0.0, pltpu.roll(v, 1, v.ndim - 1))

    def sweep(old, new, rim):
        lo, n = YO - rim, wy + 2 * rim

        def plane(t, carry):
            x = XO - rim + t
            mid = old[x, lo : lo + n]
            around = old[x + 1, lo : lo + n] + old[x - 1, lo : lo + n]
            around = around + (old[x, lo + 1 : lo + n + 1] + old[x, lo - 1 : lo + n - 1])
            around = around + (up(mid) + down(mid))
            new[x, lo : lo + n] = (around + kappa_charge * echarge[x, lo : lo + n]) / 6.0
            return carry

        lax.fori_loop(0, wx + 2 * rim, plane, 0)

    sweep(ephi, ephi1, 2)
    sweep(ephi1, ephi2, 1)

    reach = []
    for n in range(9):
        z = marks[n, 4:5].astype(jnp.int32)
        level = lax.broadcasted_iota(jnp.int32, (depth, 128), 0)
        reach.append(jnp.where(level == z, 1.0, 0.0).astype(BF16))
    rows = wx * wy
    for n in range(9):
        block = held[n].reshape(rows, 128)
        for k in range(4):
            hi, mid, low = split3(block * marks[n, k : k + 1])
            bead_rows[0, k * rows : (k + 1) * rows, n * 128 : (n + 1) * 128] = hi
            bead_rows[1, k * rows : (k + 1) * rows, n * 128 : (n + 1) * 128] = mid
            bead_rows[2, k * rows : (k + 1) * rows, n * 128 : (n + 1) * 128] = low
    everywhere = jnp.concatenate(reach, 1)
    spread = total_of([dot_t(bead_rows[p], everywhere) for p in range(3)])
    pushes[...] = spread.reshape(4, wx, wy, depth)

    def node_plane(x, carry):
        flags = flags_ref[x]
        bit = lambda b: ((flags >> b) & 1).astype(F32)
        opened = [bit(b) for b in range(6)]
        solid = bit(6) > 0.5
        phi = ephi2[XO + x, inner]
        phi_out[x] = phi
        phi_low = [ephi2[XO + x - 1, inner], ephi2[XO + x, YO - 1 : YO - 1 + wy]]
        phi_high = [ephi2[XO + x + 1, inner], ephi2[XO + x, YO + 1 : YO + 1 + wy]]
        phi_z_low, phi_z_high = pltpu.roll(phi, 1, 1), pltpu.roll(phi, depth - 1, 1)
        drift = [drift_ref[a, x] for a in range(3)]
        drift_low = [edrift[0, x, inner], edrift[1, 1 + x, YO - 1 : YO - 1 + wy]]
        drift_high = [edrift[0, x + 2, inner], edrift[1, 1 + x, YO + 1 : YO + 1 + wy]]
        drift_z_low = pltpu.roll(drift[2], 1, 1)

        def flux(lo_ion, hi_ion, lo_phi, hi_phi, lo_drift, hi_drift, gate, s):
            middle = 0.5 * (lo_ion + hi_ion)
            diffusive = -diffusion[s] * (
                (hi_ion - lo_ion) + valence[s] * middle * (hi_phi - lo_phi)
            )
            return gate * (diffusive + 0.5 * (lo_drift + hi_drift) * middle)

        both = []
        for s in range(2):
            ion = eion[s, 1 + x, inner]
            both.append(ion)
            ion_low = [eion[s, x, inner], eion[s, 1 + x, YO - 1 : YO - 1 + wy]]
            ion_high = [eion[s, x + 2, inner], eion[s, 1 + x, YO + 1 : YO + 1 + wy]]
            divergence = 0.0
            for a in range(2):
                entering = flux(
                    ion_low[a], ion, phi_low[a], phi, drift_low[a], drift[a], opened[2 * a], s
                )
                leaving = flux(
                    ion, ion_high[a], phi, phi_high[a], drift[a], drift_high[a], opened[2 * a + 1], s
                )
                divergence = divergence + (leaving - entering)
            entering = flux(
                pltpu.roll(ion, 1, 1), ion, phi_z_low, phi, drift_z_low, drift[2], opened[4], s
            )
            divergence = divergence + (pltpu.roll(entering, depth - 1, 1) - entering)
            ions_out[s, x] = ion - divergence
        charge = both[0] - both[1]

        read = []
        for i in range(19):
            sx, sy, sz = (int(c) for c in LATTICE[i])
            v = ext[i, 1 + x - sx, YO - sy : YO - sy + wy]
            read.append(v if sz == 0 else pltpu.roll(v, sz % depth, 1))
        density = total_of(read)
        inverse = 1.0 / density
        field = [
            (phi_low[0] - phi_high[0]) * 0.5,
            (phi_low[1] - phi_high[1]) * 0.5,
            (jnp.where(lanes == 0, 0.0, phi_z_low) - jnp.where(lanes == depth - 1, 0.0, phi_z_high))
            * 0.5,
        ]
        shifted = []
        for a in range(3):
            velocity = momentum(read, a) * inverse
            vels[a, x] = velocity
            force = charge * field[a] + friction * (pushes[a, x] - pushes[3, x] * velocity)
            shifted.append(velocity + tau_relax * force * inverse)
        base = 1.0 - 1.5 * (
            shifted[0] * shifted[0] + shifted[1] * shifted[1] + shifted[2] * shifted[2]
        )
        scaled = [w * density * (1.0 / tau_relax) for w in (1.0 / 3.0, 1.0 / 18.0, 1.0 / 36.0)]
        keep = 1.0 - 1.0 / tau_relax
        pops_out[0, x] = jnp.where(solid, read[0], keep * read[0] + scaled[0] * base)
        for i in range(1, 19, 2):
            along = 0.0
            for a in range(3):
                if LATTICE[i][a] != 0:
                    along = along + float(LATTICE[i][a]) * shifted[a]
            even = base + 4.5 * along * along
            odd = 3.0 * along
            scale = scaled[1] if i < 7 else scaled[2]
            pops_out[i, x] = jnp.where(
                solid, read[i + 1], keep * read[i] + scale * (even + odd)
            )
            pops_out[i + 1, x] = jnp.where(
                solid, read[i], keep * read[i + 1] + scale * (even - odd)
            )
        return carry

    lax.fori_loop(0, wx, node_plane, 0)

    parts = split3(vels[...].reshape(3 * rows, depth))
    for n in range(9):
        sampled = total_of(
            [lax.dot_general(p, reach[n], (((1,), (0,)), ((), ())), preferred_element_type=F32)
             for p in parts]
        )
        block = held[n].reshape(rows, 128)
        for k in range(3):
            part_ref[n, k : k + 1] = jnp.sum(
                block * sampled[k * rows : (k + 1) * rows], axis=0, keepdims=True
            )
        part_ref[n, 3:8] = jnp.zeros((5, 128), F32)


def local(
    shape, populations, ion_density, potential, node_flags, colloid_count, colloid_centre,
    colloid_velocity, colloid_spin, bead_cell, bead_frac, bead_weight,
):
    wx, wy, depth = potential.shape
    beads = bead_cell.shape[3]
    kp = -(-beads // CHUNK) * CHUNK
    vmem = pl.BlockSpec(memory_space=pltpu.VMEM)
    smem = pl.BlockSpec(memory_space=pltpu.SMEM)
    array = lambda *dims: jax.ShapeDtypeStruct(dims, F32)
    tall, wide = wy + 2 * YO, wx + 2
    x_rows = 8 + RADIUS * wy + 12 * wy
    y_rows = 8 + wx * 8 + 12 * wx
    c_rows = 8 + RADIUS * 8 + 8
    slabs = [array(2, x_rows, depth), array(2, y_rows, depth), array(4, c_rows, depth)]
    xs, ys, cs, own, drift, base = pl.pallas_call(
        pack_kernel,
        out_shape=slabs
        + [array(8 + wx * wy, depth), array(3, wx, wy, depth), array(6, 2, 128)],
        in_specs=[smem] * 4 + [vmem] * 6,
        out_specs=[vmem] * 6,
        scratch_shapes=[
            pltpu.VMEM((5, 2, kp), F32),
            pltpu.VMEM((6, 2, kp), F32),
            pltpu.VMEM(((wx + 2 * RADIUS) * tall, 192), F32),
            pltpu.VMEM(((wx + 2 * RADIUS) * tall, 128), F32),
        ],
    )(
        colloid_count, colloid_centre, colloid_velocity, colloid_spin, bead_cell, bead_frac,
        bead_weight, populations, ion_density, potential,
    )
    rx, ry, rc = pl.pallas_call(
        functools.partial(exchange_kernel, shape),
        out_shape=slabs,
        in_specs=[vmem] * 3,
        out_specs=[vmem] * 3,
        scratch_shapes=[pltpu.SemaphoreType.DMA((8,)), pltpu.SemaphoreType.DMA((8,))],
        compiler_params=pltpu.CompilerParams(collective_id=0, has_side_effects=True),
    )(xs, ys, cs)
    pops_next, ions_next, phi_next, parts = pl.pallas_call(
        main_kernel,
        out_shape=[
            array(*populations.shape), array(*ion_density.shape), array(*potential.shape),
            array(9, 8, 128),
        ],
        in_specs=[vmem] * 9,
        out_specs=[vmem] * 4,
        scratch_shapes=[
            pltpu.VMEM((19, wide, tall, depth), F32),
            pltpu.VMEM((2, wide, tall, depth), F32),
            pltpu.VMEM((wx + 2 * XO, tall, depth), F32),
            pltpu.VMEM((2, wide, tall, depth), F32),
            pltpu.VMEM((wx + 2 * XO, tall, depth), F32),
            pltpu.VMEM((wx + 2 * XO, tall, depth), F32),
            pltpu.VMEM((wx + 2 * XO, tall, depth), F32),
            pltpu.VMEM((9, wx, wy, 128), F32),
            pltpu.VMEM((9, 8, 128), F32),
            pltpu.VMEM((3, 4 * wx * wy, 9 * 128), BF16),
            pltpu.VMEM((4, wx, wy, depth), F32),
            pltpu.VMEM((3, wx, wy, depth), F32),
        ],
    )(populations, ion_density, potential, node_flags, drift, own, rx, ry, rc)
    kick = pl.pallas_call(
        functools.partial(return_kernel, shape, float(beads)),
        out_shape=array(6, 2, 128),
        in_specs=[vmem] * 2,
        out_specs=vmem,
        scratch_shapes=[
            pltpu.VMEM((8, 8, 128), F32),
            pltpu.SemaphoreType.DMA((8,)),
            pltpu.SemaphoreType.DMA((8,)),
        ],
        compiler_params=pltpu.CompilerParams(collective_id=1, has_side_effects=True),
    )(parts, base)
    return pops_next, ions_next, phi_next, kick[:, :, 0].reshape(6, 1, 1, 2)


def solution(mesh):
    in_specs = (
        P(None, "gx", "gy", None),
        P(None, "gx", "gy", None),
        P("gx", "gy", None),
        P("gx", "gy", None),
        P("gx", "gy"),
        P(None, "gx", "gy", None),
        P(None, "gx", "gy", None),
        P(None, "gx", "gy", None),
        P("gx", "gy", None, None),
        P(None, "gx", "gy", None, None),
        P("gx", "gy", None, None),
    )
    out_specs = (
        P(None, "gx", "gy", None),
        P(None, "gx", "gy", None),
        P("gx", "gy", None),
        P(None, "gx", "gy", None),
    )
    shape = (mesh.shape["gx"], mesh.shape["gy"])
    return jax.shard_map(
        functools.partial(local, shape), mesh=mesh, in_specs=in_specs, out_specs=out_specs,
        check_vma=False,
    )
```

```python
import functools

import jax
import jax.numpy as jnp
import numpy as np
from jax import lax
from jax.experimental import pallas as pl
from jax.experimental.pallas import tpu as pltpu
from jax.sharding import PartitionSpec as P

RADIUS = 6
SIDE = 2 * RADIUS + 1
YO = 8
XO = 3
MESH = pl.DeviceIdType.MESH
F32 = jnp.float32
BF16 = jnp.bfloat16

LATTICE = np.array(
    [
        [0, 0, 0],
        [1, 0, 0],
        [-1, 0, 0],
        [0, 1, 0],
        [0, -1, 0],
        [0, 0, 1],
        [0, 0, -1],
        [1, 1, 0],
        [-1, -1, 0],
        [1, -1, 0],
        [-1, 1, 0],
        [1, 0, 1],
        [-1, 0, -1],
        [1, 0, -1],
        [-1, 0, 1],
        [0, 1, 1],
        [0, -1, -1],
        [0, 1, -1],
        [0, -1, 1],
    ]
)
OPPOSITE = [0, 2, 1, 4, 3, 6, 5, 8, 7, 10, 9, 12, 11, 14, 13, 16, 15, 18, 17]
tau_relax = 0.8
kappa_charge = 0.5
friction = 4.0
diffusion = (0.12, 0.15)
valence = (1.0, -1.0)
X_DIRS = [(1, 0), (-1, 0)]
Y_DIRS = [(0, 1), (0, -1)]
C_DIRS = [(1, 1), (1, -1), (-1, 1), (-1, -1)]
DIRS = X_DIRS + Y_DIRS + C_DIRS


def lattice_weight(i):
    if i == 0:
        return 1.0 / 3.0
    if i < 7:
        return 1.0 / 18.0
    return 1.0 / 36.0


def links(a, sign):
    return [i for i in range(19) if LATTICE[i][a] == sign]


def corner_link(sx, sy):
    return [i for i in range(19) if tuple(LATTICE[i]) == (sx, sy, 0)][0]


def total_of(terms):
    terms = list(terms)
    while len(terms) > 1:
        terms = [
            terms[j] + terms[j + 1] if j + 1 < len(terms) else terms[j]
            for j in range(0, len(terms), 2)
        ]
    return terms[0]


def momentum(pops, a):
    return total_of(pops[i] for i in links(a, 1)) - total_of(pops[i] for i in links(a, -1))


def layer(s, depth, width):
    return width - 1 - depth if s > 0 else depth


def halo(s, depth, width):
    return -1 - depth if s > 0 else width + depth


def split3(v):
    hi = v.astype(BF16)
    rest = v - hi.astype(F32)
    mid = rest.astype(BF16)
    low = (rest - mid.astype(F32)).astype(BF16)
    return hi, mid, low


def dot_t(a, b):
    return lax.dot_general(a, b, (((1,), (1,)), ((), ())), preferred_element_type=F32)


def bead_span_x(sx, width):
    if sx > 0:
        return RADIUS + width, RADIUS, 0
    if sx < 0:
        return 0, RADIUS, width - RADIUS
    return RADIUS, width, 0


def bead_span_y(sy, width):
    if sy > 0:
        return YO + width, 8, 0
    if sy < 0:
        return 0, 8, width - 8
    return YO, width, 0


def neighbour(shape, sx, sy):
    nx, ny = shape
    return (
        lax.rem(lax.axis_index("gx") + (sx + nx), nx),
        lax.rem(lax.axis_index("gy") + (sy + ny), ny),
    )


def send_all(shape, sources, targets, send, recv, way):
    copies = []
    for d, (sx, sy) in enumerate(DIRS):
        copies.append(
            pltpu.make_async_remote_copy(
                src_ref=sources[d], dst_ref=targets[d], send_sem=send.at[d], recv_sem=recv.at[d],
                device_id=neighbour(shape, way * sx, way * sy), device_id_type=MESH,
            )
        )
    for copy in copies:
        copy.start()
    return copies


def eight(x, y, c):
    return [x.at[0], x.at[1], y.at[0], y.at[1]] + [c.at[j] for j in range(4)]


def first_kernel(
    shape, count_ref, centre_ref, vel_ref, spin_ref, cell_ref, frac_ref, weight_ref, pops_ref,
    ions_ref, phi_ref, flags_ref,
    read_out, shifted_out, ions_out, phi_out, kick_ref,
    xs, ys, cs, rx, ry, rc, bxs, bys, bcs, bxr, byr, bcr, own,
    drift_ref, beads, codes, acc, field,
    ext, eion, echarge, edrift, ephi, ephi1, ephi2, held, marks, bead_rows, pushes, vels, dens,
    part, got, send, recv,
):
    wx, wy, depth = phi_ref.shape
    nb = cell_ref.shape[3]
    kp = beads.shape[2]
    chunk = kp // 2
    tall = 2 * YO + wy
    span_x = wx + 2 * RADIUS
    inner = slice(YO, YO + wy)
    lanes = lax.broadcasted_iota(jnp.int32, (1, depth), 1)
    rows = wx * wy

    barrier = pltpu.get_barrier_semaphore()
    for sx, sy in DIRS:
        pl.semaphore_signal(barrier, inc=1, device_id=neighbour(shape, sx, sy), device_id_type=MESH)

    def drift_plane(x, carry):
        pops = [pops_ref[i, x] for i in range(19)]
        inv = 1.0 / total_of(pops)
        for a in range(3):
            drift_ref[a, x] = momentum(pops, a) * inv
        return carry

    lax.fori_loop(0, wx, drift_plane, 0)

    def charge_at(x, y):
        return ions_ref[0, x, y] - ions_ref[1, x, y]

    for j, (sx, _) in enumerate(X_DIRS):
        out, at, edge = xs.at[j], 0, layer(sx, 0, wx)
        parts = [pops_ref[i, edge] for i in links(0, sx)]
        parts += [ions_ref[0, edge], ions_ref[1, edge], charge_at(layer(sx, 1, wx), slice(None))]
        parts += [phi_ref[layer(sx, l, wx)] for l in range(3)] + [drift_ref[0, edge]]
        for row in parts:
            out[at : at + wy] = row
            at += wy
    for j, (_, sy) in enumerate(Y_DIRS):
        out, at, edge = ys.at[j], 0, layer(sy, 0, wy)
        parts = [pops_ref[i, :, edge] for i in links(1, sy)]
        parts += [ions_ref[0, :, edge], ions_ref[1, :, edge]]
        parts += [charge_at(slice(None), layer(sy, 1, wy))]
        parts += [phi_ref[:, layer(sy, l, wy)] for l in range(3)] + [drift_ref[1, :, edge]]
        for row in parts:
            out[at : at + wx] = row
            at += wx
    for j, (sx, sy) in enumerate(C_DIRS):
        out = cs.at[j]
        ex, ey = layer(sx, 0, wx), layer(sy, 0, wy)
        parts = [
            pops_ref[corner_link(sx, sy), ex, ey],
            charge_at(ex, ey),
            phi_ref[ex, ey],
            phi_ref[layer(sx, 1, wx), ey],
            phi_ref[ex, layer(sy, 1, wy)],
        ]
        for at, row in enumerate(parts):
            out[at] = row
        out[5:8] = jnp.zeros((3, depth), F32)
    pl.semaphore_wait(barrier, len(DIRS))
    halos = send_all(
        shape, eight(xs, ys, cs), eight(rx, ry, rc), send.at[0], recv.at[0], 1
    )

    beads[...] = jnp.zeros_like(beads)
    beads[0, :, :nb] = cell_ref[0, 0].astype(F32)
    for k in range(3):
        beads[1 + k, :, :nb] = frac_ref[k, 0, 0]
    beads[4, :, :nb] = weight_ref[0, 0]
    first = lax.broadcasted_iota(jnp.int32, (2, kp), 0) == 0
    count = count_ref[0, 0]

    def pick(ref, k):
        return jnp.where(first, ref[0, k], ref[1, k])

    cell = beads[0]
    ix = jnp.floor((cell + 0.5) * (1.0 / (SIDE * SIDE)))
    rest = cell - ix * (SIDE * SIDE)
    iy = jnp.floor((rest + 0.5) * (1.0 / SIDE))
    iz = rest - iy * SIDE
    slot = jnp.where(first, 0, 1)
    weight = jnp.where(slot < count, beads[4], 0.0)
    lever = [idx - RADIUS + beads[1 + k] for k, idx in enumerate((ix, iy, iz))]
    local_y = [lax.rem(centre_ref[s, 1], wy).astype(F32) for s in range(2)]
    py = iy + jnp.where(first, local_y[0], local_y[1]) + (YO - RADIUS)
    codes[0] = ix * tall + py
    codes[1] = iz
    codes[2] = weight
    for k in range(3):
        codes[3 + k] = weight * lever[k]
    acc[0 : wx - 1] = jnp.zeros((wx - 1, tall, 192), F32)
    acc[wx - 1 + SIDE :] = jnp.zeros((wx - 1, tall, 192), F32)
    for s in range(2):

        def cells(c):
            span = pl.ds(pl.multiple_of(c * chunk, 128), chunk)
            code = codes[0, s : s + 1, span].astype(jnp.int32)
            node = lax.broadcasted_iota(jnp.int32, (SIDE * tall, chunk), 0)
            place = jnp.where(node == code, 1.0, 0.0).astype(BF16)
            level = codes[1, s : s + 1, span].astype(jnp.int32)
            at_level = lax.broadcasted_iota(jnp.int32, (16, chunk), 0) == level
            values = jnp.concatenate(
                [jnp.where(at_level, codes[2 + q, s : s + 1, span], 0.0) for q in range(4)], 0
            )
            return dot_t(place, jnp.concatenate(split3(values), 0)).reshape(SIDE, tall, 192)

        box = slice(wx - 1, wx - 1 + SIDE)
        acc[box] = cells(0)
        acc[box] += cells(1)
        offset = wx - 1 - lax.rem(centre_ref[s, 0], wx)
        for x in range(span_x):
            plane = acc[offset + x]
            field[x * tall : (x + 1) * tall, 64 * s : 64 * s + 64] = (
                plane[:, 0:64] + plane[:, 64:128] + plane[:, 128:192]
            )

    lane = lax.broadcasted_iota(jnp.int32, (1, 128), 1)
    lane_slot = lane // 64
    channel = (lane // 16) % 4
    by_slot = lambda ref, k: jnp.where(lane_slot == 0, ref[0, k], ref[1, k])
    v = [by_slot(vel_ref, k) for k in range(3)]
    w = [by_slot(spin_ref, k) for k in range(3)]
    zero = jnp.zeros((1, 128), F32)

    def four(*terms):
        out = zero
        for q, row in enumerate(terms):
            out = jnp.where(channel == q, row, out)
        return out

    constants = jnp.concatenate(
        [
            four(v[0], zero, -w[2], w[1]),
            four(v[1], w[2], zero, -w[0]),
            four(v[2], -w[1], w[0], zero),
            four(zero + 1.0, zero, zero, zero),
            by_slot(centre_ref, 2).astype(F32) + (lane % 16 - RADIUS).astype(F32),
            zero,
            zero,
            zero,
        ],
        0,
    )

    def put_beads(ref, sx, sy):
        ref[0:8] = constants
        x0, nx, _ = bead_span_x(sx, wx)
        y0, ny, _ = bead_span_y(sy, wy)
        for x in range(nx):
            start = (x0 + x) * tall + y0
            ref[8 + x * ny : 8 + (x + 1) * ny] = field[start : start + ny]

    for ref, (sx, sy) in zip(eight(bxs, bys, bcs), DIRS):
        put_beads(ref, sx, sy)
    put_beads(own, 0, 0)
    spheres = send_all(
        shape, eight(bxs, bys, bcs), eight(bxr, byr, bcr), send.at[1], recv.at[1], 1
    )

    spread_vel = [pick(vel_ref, k) for k in range(3)]
    spin = [pick(spin_ref, k) for k in range(3)]
    cross = lambda p, q: [p[1] * q[2] - p[2] * q[1], p[2] * q[0] - p[0] * q[2], p[0] * q[1] - p[1] * q[0]]
    turn = cross(spin, lever)
    push = [weight * (spread_vel[k] + turn[k]) for k in range(3)]
    twist = cross(lever, push)
    known = [jnp.sum(t, axis=1, keepdims=True) for t in push + twist]

    for i in range(19):
        ext[i, 1 : 1 + wx, inner] = pops_ref[i]
    for s in range(2):
        eion[s, 1 : 1 + wx, inner] = ions_ref[s]
    echarge[XO : XO + wx, inner] = ions_ref[0] - ions_ref[1]
    ephi[XO : XO + wx, inner] = phi_ref[...]
    for a in range(2):
        edrift[a, 1 : 1 + wx, inner] = drift_ref[a]
    held[...] = jnp.zeros_like(held)
    for copy in halos:
        copy.wait()
    for j, (sx, _) in enumerate(X_DIRS):
        src, at, edge = rx.at[j], 0, 1 + halo(sx, 0, wx)
        for i in links(0, sx):
            ext[i, edge, inner] = src[at : at + wy]
            at += wy
        for s in range(2):
            eion[s, edge, inner] = src[at : at + wy]
            at += wy
        echarge[XO + halo(sx, 0, wx), inner] = eion[0, edge, inner] - eion[1, edge, inner]
        echarge[XO + halo(sx, 1, wx), inner] = src[at : at + wy]
        at += wy
        for l in range(3):
            ephi[XO + halo(sx, l, wx), inner] = src[at : at + wy]
            at += wy
        edrift[0, edge, inner] = src[at : at + wy]
    for j, (_, sy) in enumerate(Y_DIRS):
        src, at, edge = ry.at[j], 0, YO + halo(sy, 0, wy)
        for i in links(1, sy):
            ext[i, 1 : 1 + wx, edge] = src[at : at + wx]
            at += wx
        ion0, ion1 = src[at : at + wx], src[at + wx : at + 2 * wx]
        eion[0, 1 : 1 + wx, edge] = ion0
        eion[1, 1 : 1 + wx, edge] = ion1
        at += 2 * wx
        echarge[XO : XO + wx, edge] = ion0 - ion1
        echarge[XO : XO + wx, YO + halo(sy, 1, wy)] = src[at : at + wx]
        at += wx
        for l in range(3):
            ephi[XO : XO + wx, YO + halo(sy, l, wy)] = src[at : at + wx]
            at += wx
        edrift[1, 1 : 1 + wx, edge] = src[at : at + wx]
    for j, (sx, sy) in enumerate(C_DIRS):
        src = rc.at[j]
        hx, hy = halo(sx, 0, wx), YO + halo(sy, 0, wy)
        ext[corner_link(sx, sy), 1 + hx, hy] = src[0]
        echarge[XO + hx, hy] = src[1]
        ephi[XO + hx, hy] = src[2]
        ephi[XO + halo(sx, 1, wx), hy] = src[3]
        ephi[XO + hx, YO + halo(sy, 1, wy)] = src[4]

    def velocity_plane(x, carry):
        read = []
        for i in range(19):
            sx, sy, sz = (int(c) for c in LATTICE[i])
            v = ext[i, 1 + x - sx, YO - sy : YO - sy + wy]
            read.append(v if sz == 0 else pltpu.roll(v, sz % depth, 1))
            read_out[i, x] = read[i]
        inverse = 1.0 / total_of(read)
        dens[x] = inverse
        for a in range(3):
            vels[a, x] = momentum(read, a) * inverse
        return carry

    lax.fori_loop(0, wx, velocity_plane, 0)

    def up(v):
        return jnp.where(lanes == depth - 1, 0.0, pltpu.roll(v, depth - 1, v.ndim - 1))

    def down(v):
        return jnp.where(lanes == 0, 0.0, pltpu.roll(v, 1, v.ndim - 1))

    def sweep(old, new, rim):
        lo, n = YO - rim, wy + 2 * rim

        def plane(t, carry):
            x = XO - rim + t
            mid = old[x, lo : lo + n]
            around = old[x + 1, lo : lo + n] + old[x - 1, lo : lo + n]
            around = around + (old[x, lo + 1 : lo + n + 1] + old[x, lo - 1 : lo + n - 1])
            around = around + (up(mid) + down(mid))
            new[x, lo : lo + n] = (around + kappa_charge * echarge[x, lo : lo + n]) / 6.0
            return carry

        lax.fori_loop(0, wx + 2 * rim, plane, 0)

    sweep(ephi, ephi1, 2)
    sweep(ephi1, ephi2, 1)

    def ion_plane(x, carry):
        flags = flags_ref[x]
        bit = lambda b: ((flags >> b) & 1).astype(F32)
        opened = [bit(b) for b in range(6)]
        phi = ephi2[XO + x, inner]
        phi_out[x] = phi
        phi_low = [ephi2[XO + x - 1, inner], ephi2[XO + x, YO - 1 : YO - 1 + wy]]
        phi_high = [ephi2[XO + x + 1, inner], ephi2[XO + x, YO + 1 : YO + 1 + wy]]
        phi_z_low, phi_z_high = pltpu.roll(phi, 1, 1), pltpu.roll(phi, depth - 1, 1)
        drift = [drift_ref[a, x] for a in range(3)]
        drift_low = [edrift[0, x, inner], edrift[1, 1 + x, YO - 1 : YO - 1 + wy]]
        drift_high = [edrift[0, x + 2, inner], edrift[1, 1 + x, YO + 1 : YO + 1 + wy]]
        drift_z_low = pltpu.roll(drift[2], 1, 1)

        def flux(lo_ion, hi_ion, lo_phi, hi_phi, lo_drift, hi_drift, gate, s):
            middle = 0.5 * (lo_ion + hi_ion)
            diffusive = -diffusion[s] * (
                (hi_ion - lo_ion) + valence[s] * middle * (hi_phi - lo_phi)
            )
            return gate * (diffusive + 0.5 * (lo_drift + hi_drift) * middle)

        both = []
        for s in range(2):
            ion = eion[s, 1 + x, inner]
            both.append(ion)
            ion_low = [eion[s, x, inner], eion[s, 1 + x, YO - 1 : YO - 1 + wy]]
            ion_high = [eion[s, x + 2, inner], eion[s, 1 + x, YO + 1 : YO + 1 + wy]]
            divergence = 0.0
            for a in range(2):
                entering = flux(
                    ion_low[a], ion, phi_low[a], phi, drift_low[a], drift[a], opened[2 * a], s
                )
                leaving = flux(
                    ion, ion_high[a], phi, phi_high[a], drift[a], drift_high[a], opened[2 * a + 1], s
                )
                divergence = divergence + (leaving - entering)
            entering = flux(
                pltpu.roll(ion, 1, 1), ion, phi_z_low, phi, drift_z_low, drift[2], opened[4], s
            )
            divergence = divergence + (pltpu.roll(entering, depth - 1, 1) - entering)
            ions_out[s, x] = ion - divergence
        charge = both[0] - both[1]

        field_x = (phi_low[0] - phi_high[0]) * 0.5
        field_y = (phi_low[1] - phi_high[1]) * 0.5
        field_z = (
            jnp.where(lanes == 0, 0.0, phi_z_low) - jnp.where(lanes == depth - 1, 0.0, phi_z_high)
        ) * 0.5
        scale = tau_relax * charge * dens[x]
        for a, e in enumerate((field_x, field_y, field_z)):
            shifted_out[a, x] = vels[a, x] + scale * e
        return carry

    lax.fori_loop(0, wx, ion_plane, 0)

    for copy in spheres:
        copy.wait()
    for n, (ref, (sx, sy)) in enumerate(zip([own] + eight(bxr, byr, bcr), [(0, 0)] + DIRS)):
        _, nx, tx = bead_span_x(sx, wx)
        _, ny, ty = bead_span_y(sy, wy)
        marks[n] = ref[0:8]
        for x in range(nx):
            held[n, tx + x, ty : ty + ny] = ref[8 + x * ny : 8 + (x + 1) * ny]
    reach = []
    for n in range(9):
        z = marks[n, 4:5].astype(jnp.int32)
        level = lax.broadcasted_iota(jnp.int32, (depth, 128), 0)
        reach.append(jnp.where(level == z, 1.0, 0.0).astype(BF16))

    parts = split3(vels[...].reshape(3 * rows, depth))
    for n in range(9):
        sampled = total_of(
            [lax.dot_general(p, reach[n], (((1,), (0,)), ((), ())), preferred_element_type=F32)
             for p in parts]
        )
        block = held[n].reshape(rows, 128)
        for k in range(3):
            part[n, k : k + 1] = jnp.sum(
                block * sampled[k * rows : (k + 1) * rows], axis=0, keepdims=True
            )
        part[n, 3:8] = jnp.zeros((5, 128), F32)
    backs = send_all(
        shape, [part.at[d + 1] for d in range(8)], [got.at[d] for d in range(8)],
        send.at[2], recv.at[2], -1,
    )

    for n in range(9):
        block = held[n].reshape(rows, 128)
        for k in range(4):
            for p, piece in enumerate(split3(block * marks[n, k : k + 1])):
                bead_rows[p, k * rows : (k + 1) * rows, n * 128 : (n + 1) * 128] = piece
    everywhere = jnp.concatenate(reach, 1)
    spread = total_of([dot_t(bead_rows[p], everywhere) for p in range(3)])
    pushes[...] = spread.reshape(4, wx, wy, depth)
    scale = (tau_relax * friction) * dens[...]
    for a in range(3):
        shifted_out[a] += scale * (pushes[a] - pushes[3] * vels[a])

    for copy in backs:
        copy.wait()
    whole = total_of([part[0]] + [got[d] for d in range(8)])
    group = lax.broadcasted_iota(jnp.int32, (8, 128), 1) // 16
    for s in range(2):
        m = [
            jnp.sum(jnp.where(group == 4 * s + q, whole, 0.0), axis=1, keepdims=True)
            for q in range(4)
        ]
        mean = [m[0][k : k + 1] for k in range(3)]
        lev = [[m[1 + a][k : k + 1] for k in range(3)] for a in range(3)]
        turned = [lev[1][2] - lev[2][1], lev[2][0] - lev[0][2], lev[0][1] - lev[1][0]]
        for k, t in enumerate(mean + turned):
            kick_ref[s : s + 1, k : k + 1] = (known[k][s : s + 1] - t) * (-friction / nb)


def second_kernel(
    read_ref, shifted_ref, flags_ref, ions_ref, phi_ref, kick_ref,
    pops_out, ions_out, phi_out, kick_out,
):
    kick_out[...] = kick_ref[...]

    def collide_plane(x, carry):
        phi_out[x] = phi_ref[x]
        for s in range(2):
            ions_out[s, x] = ions_ref[s, x]
        solid = ((flags_ref[x] >> 6) & 1) == 1
        read = [read_ref[i, x] for i in range(19)]
        density = total_of(read)
        shifted = [shifted_ref[a, x] for a in range(3)]
        base = 1.0 - 1.5 * (
            shifted[0] * shifted[0] + shifted[1] * shifted[1] + shifted[2] * shifted[2]
        )
        scaled = [w * density * (1.0 / tau_relax) for w in (1.0 / 3.0, 1.0 / 18.0, 1.0 / 36.0)]
        keep = 1.0 - 1.0 / tau_relax
        pops_out[0, x] = jnp.where(solid, read[0], keep * read[0] + scaled[0] * base)
        for i in range(1, 19, 2):
            along = 0.0
            for a in range(3):
                if LATTICE[i][a] != 0:
                    along = along + float(LATTICE[i][a]) * shifted[a]
            even = base + 4.5 * along * along
            odd = 3.0 * along
            scale = scaled[1] if i < 7 else scaled[2]
            pops_out[i, x] = jnp.where(
                solid, read[i + 1], keep * read[i] + scale * (even + odd)
            )
            pops_out[i + 1, x] = jnp.where(
                solid, read[i], keep * read[i + 1] + scale * (even - odd)
            )
        return carry

    lax.fori_loop(0, phi_ref.shape[0], collide_plane, 0)


def local(
    shape, populations, ion_density, potential, node_flags, colloid_count, colloid_centre,
    colloid_velocity, colloid_spin, bead_cell, bead_frac, bead_weight,
):
    wx, wy, depth = potential.shape
    kp = -(-bead_cell.shape[3] // 256) * 256
    vmem = pl.BlockSpec(memory_space=pltpu.VMEM)
    smem = pl.BlockSpec(memory_space=pltpu.SMEM)
    array = lambda *dims: jax.ShapeDtypeStruct(dims, F32)
    mem = lambda *dims: pltpu.VMEM(dims, F32)
    by_slot = lambda a: jnp.transpose(a, (1, 2, 3, 0)).reshape(a.shape[3], a.shape[0])
    tall, wide, far = wy + 2 * YO, wx + 2, wx + 2 * XO
    slabs = [mem(2, 12 * wy, depth), mem(2, 12 * wx, depth), mem(4, 8, depth)]
    balls = [mem(2, 8 + RADIUS * wy, 128), mem(2, 8 + wx * 8, 128), mem(4, 8 + RADIUS * 8, 128)]
    read, shifted, ions, phi, kick = pl.pallas_call(
        functools.partial(first_kernel, shape),
        out_shape=[
            array(*populations.shape), array(3, wx, wy, depth), array(*ion_density.shape),
            array(*potential.shape), array(2, 6),
        ],
        in_specs=[smem] * 4 + [vmem] * 7,
        out_specs=[vmem] * 5,
        scratch_shapes=slabs + slabs + balls + balls + [
            mem(8 + wx * wy, 128),
            mem(3, wx, wy, depth),
            mem(5, 2, kp),
            mem(6, 2, kp),
            mem(SIDE + 2 * (wx - 1), tall, 192),
            mem((wx + 2 * RADIUS) * tall, 128),
            mem(19, wide, tall, depth),
            mem(2, wide, tall, depth),
            mem(far, tall, depth),
            mem(2, wide, tall, depth),
            mem(far, tall, depth),
            mem(far, tall, depth),
            mem(far, tall, depth),
            mem(9, wx, wy, 128),
            mem(9, 8, 128),
            pltpu.VMEM((3, 4 * wx * wy, 9 * 128), BF16),
            mem(4, wx, wy, depth),
            mem(3, wx, wy, depth),
            mem(wx, wy, depth),
            mem(9, 8, 128),
            mem(8, 8, 128),
            pltpu.SemaphoreType.DMA((3, 8)),
            pltpu.SemaphoreType.DMA((3, 8)),
        ],
        compiler_params=pltpu.CompilerParams(collective_id=0, has_side_effects=True),
    )(
        colloid_count, by_slot(colloid_centre), by_slot(colloid_velocity), by_slot(colloid_spin),
        bead_cell, bead_frac, bead_weight, populations, ion_density, potential, node_flags,
    )
    pops_next, ions_next, phi_next, kick = pl.pallas_call(
        second_kernel,
        out_shape=[
            array(*populations.shape), array(*ion_density.shape), array(*potential.shape),
            array(2, 6),
        ],
        in_specs=[vmem] * 6,
        out_specs=[vmem] * 4,
    )(read, shifted, node_flags, ions, phi, kick)
    return pops_next, ions_next, phi_next, jnp.transpose(kick.reshape(1, 1, 2, 6), (3, 0, 1, 2))


def solution(mesh):
    in_specs = (
        P(None, "gx", "gy", None),
        P(None, "gx", "gy", None),
        P("gx", "gy", None),
        P("gx", "gy", None),
        P("gx", "gy"),
        P(None, "gx", "gy", None),
        P(None, "gx", "gy", None),
        P(None, "gx", "gy", None),
        P("gx", "gy", None, None),
        P(None, "gx", "gy", None, None),
        P("gx", "gy", None, None),
    )
    out_specs = (
        P(None, "gx", "gy", None),
        P(None, "gx", "gy", None),
        P("gx", "gy", None),
        P(None, "gx", "gy", None),
    )
    shape = (mesh.shape["gx"], mesh.shape["gy"])
    return jax.shard_map(
        functools.partial(local, shape), mesh=mesh, in_specs=in_specs, out_specs=out_specs,
        check_vma=False,
    )
```

```python
import functools

import jax
import jax.numpy as jnp
import numpy as np
from jax import lax
from jax.experimental import pallas as pl
from jax.experimental.pallas import tpu as pltpu
from jax.sharding import PartitionSpec as P

RADIUS = 6
SIDE = 2 * RADIUS + 1
YO = 8
XO = 3
MESH = pl.DeviceIdType.MESH
F32 = jnp.float32
BF16 = jnp.bfloat16

LATTICE = np.array(
    [
        [0, 0, 0],
        [1, 0, 0],
        [-1, 0, 0],
        [0, 1, 0],
        [0, -1, 0],
        [0, 0, 1],
        [0, 0, -1],
        [1, 1, 0],
        [-1, -1, 0],
        [1, -1, 0],
        [-1, 1, 0],
        [1, 0, 1],
        [-1, 0, -1],
        [1, 0, -1],
        [-1, 0, 1],
        [0, 1, 1],
        [0, -1, -1],
        [0, 1, -1],
        [0, -1, 1],
    ]
)
OPPOSITE = [0, 2, 1, 4, 3, 6, 5, 8, 7, 10, 9, 12, 11, 14, 13, 16, 15, 18, 17]
tau_relax = 0.8
kappa_charge = 0.5
friction = 4.0
diffusion = (0.12, 0.15)
valence = (1.0, -1.0)
X_DIRS = [(1, 0), (-1, 0)]
Y_DIRS = [(0, 1), (0, -1)]
C_DIRS = [(1, 1), (1, -1), (-1, 1), (-1, -1)]
DIRS = X_DIRS + Y_DIRS + C_DIRS


def lattice_weight(i):
    if i == 0:
        return 1.0 / 3.0
    if i < 7:
        return 1.0 / 18.0
    return 1.0 / 36.0


def links(a, sign):
    return [i for i in range(19) if LATTICE[i][a] == sign]


def corner_link(sx, sy):
    return [i for i in range(19) if tuple(LATTICE[i]) == (sx, sy, 0)][0]


def total_of(terms):
    terms = list(terms)
    while len(terms) > 1:
        terms = [
            terms[j] + terms[j + 1] if j + 1 < len(terms) else terms[j]
            for j in range(0, len(terms), 2)
        ]
    return terms[0]


def momentum(pops, a):
    return total_of(pops[i] for i in links(a, 1)) - total_of(pops[i] for i in links(a, -1))


def layer(s, depth, width):
    return width - 1 - depth if s > 0 else depth


def halo(s, depth, width):
    return -1 - depth if s > 0 else width + depth


def split3(v):
    hi = v.astype(BF16)
    rest = v - hi.astype(F32)
    mid = rest.astype(BF16)
    low = (rest - mid.astype(F32)).astype(BF16)
    return hi, mid, low


def dot_t(a, b):
    return lax.dot_general(a, b, (((1,), (1,)), ((), ())), preferred_element_type=F32)


def bead_span_x(sx, width):
    if sx > 0:
        return RADIUS + width, RADIUS, 0
    if sx < 0:
        return 0, RADIUS, width - RADIUS
    return RADIUS, width, 0


def bead_span_y(sy, width):
    if sy > 0:
        return YO + width, 8, 0
    if sy < 0:
        return 0, 8, width - 8
    return YO, width, 0


def neighbour(shape, sx, sy):
    nx, ny = shape
    return (
        lax.rem(lax.axis_index("gx") + (sx + nx), nx),
        lax.rem(lax.axis_index("gy") + (sy + ny), ny),
    )


def send_all(shape, sources, targets, send, recv, way):
    copies = []
    for d, (sx, sy) in enumerate(DIRS):
        copies.append(
            pltpu.make_async_remote_copy(
                src_ref=sources[d], dst_ref=targets[d], send_sem=send.at[d], recv_sem=recv.at[d],
                device_id=neighbour(shape, way * sx, way * sy), device_id_type=MESH,
            )
        )
    for copy in copies:
        copy.start()
    return copies


def eight(x, y, c):
    return [x.at[0], x.at[1], y.at[0], y.at[1]] + [c.at[j] for j in range(4)]


def first_kernel(
    shape, count_ref, centre_ref, vel_ref, spin_ref, cell_ref, frac_ref, weight_ref, pops_ref,
    ions_ref, phi_ref, flags_ref,
    read_out, shifted_out, ions_out, phi_out, kick_ref,
    xs, ys, cs, rx, ry, rc, bxs, bys, bcs, bxr, byr, bcr, own,
    drift_ref, beads, codes, acc, field,
    ext, eion, echarge, edrift, ephi, ephi1, ephi2, held, marks, bead_rows, pushes, vels, dens,
    part, got, streamed, send, recv, local_sem,
):
    wx, wy, depth = phi_ref.shape
    nb = cell_ref.shape[3]
    kp = beads.shape[2]
    chunk = kp // 2
    tall = 2 * YO + wy
    span_x = wx + 2 * RADIUS
    inner = slice(YO, YO + wy)
    lanes = lax.broadcasted_iota(jnp.int32, (1, depth), 1)
    rows = wx * wy

    barrier = pltpu.get_barrier_semaphore()
    for sx, sy in DIRS:
        pl.semaphore_signal(barrier, inc=1, device_id=neighbour(shape, sx, sy), device_id_type=MESH)

    load = pltpu.make_async_copy(pops_ref, ext.at[:, 1 : 1 + wx, inner], local_sem.at[0])
    load.start()

    beads[...] = jnp.zeros_like(beads)
    beads[0, :, :nb] = cell_ref[0, 0].astype(F32)
    for k in range(3):
        beads[1 + k, :, :nb] = frac_ref[k, 0, 0]
    beads[4, :, :nb] = weight_ref[0, 0]
    first = lax.broadcasted_iota(jnp.int32, (2, kp), 0) == 0
    count = count_ref[0, 0]

    def pick(ref, k):
        return jnp.where(first, ref[0, k], ref[1, k])

    cell = beads[0]
    ix = jnp.floor((cell + 0.5) * (1.0 / (SIDE * SIDE)))
    rest = cell - ix * (SIDE * SIDE)
    iy = jnp.floor((rest + 0.5) * (1.0 / SIDE))
    iz = rest - iy * SIDE
    slot = jnp.where(first, 0, 1)
    weight = jnp.where(slot < count, beads[4], 0.0)
    lever = [idx - RADIUS + beads[1 + k] for k, idx in enumerate((ix, iy, iz))]
    local_y = [lax.rem(centre_ref[s, 1], wy).astype(F32) for s in range(2)]
    py = iy + jnp.where(first, local_y[0], local_y[1]) + (YO - RADIUS)
    codes[0] = ix * tall + py
    codes[1] = iz
    codes[2] = weight
    for k in range(3):
        codes[3 + k] = weight * lever[k]
    acc[0 : wx - 1] = jnp.zeros((wx - 1, tall, 192), F32)
    acc[wx - 1 + SIDE :] = jnp.zeros((wx - 1, tall, 192), F32)
    for s in range(2):

        def cells(c):
            span = pl.ds(pl.multiple_of(c * chunk, 128), chunk)
            code = codes[0, s : s + 1, span].astype(jnp.int32)
            node = lax.broadcasted_iota(jnp.int32, (SIDE * tall, chunk), 0)
            place = jnp.where(node == code, 1.0, 0.0).astype(BF16)
            level = codes[1, s : s + 1, span].astype(jnp.int32)
            at_level = lax.broadcasted_iota(jnp.int32, (16, chunk), 0) == level
            values = jnp.concatenate(
                [jnp.where(at_level, codes[2 + q, s : s + 1, span], 0.0) for q in range(4)], 0
            )
            return dot_t(place, jnp.concatenate(split3(values), 0)).reshape(SIDE, tall, 192)

        box = slice(wx - 1, wx - 1 + SIDE)
        acc[box] = cells(0)
        acc[box] += cells(1)
        offset = wx - 1 - lax.rem(centre_ref[s, 0], wx)
        for x in range(span_x):
            plane = acc[offset + x]
            field[x * tall : (x + 1) * tall, 64 * s : 64 * s + 64] = (
                plane[:, 0:64] + plane[:, 64:128] + plane[:, 128:192]
            )

    lane = lax.broadcasted_iota(jnp.int32, (1, 128), 1)
    lane_slot = lane // 64
    channel = (lane // 16) % 4
    by_slot = lambda ref, k: jnp.where(lane_slot == 0, ref[0, k], ref[1, k])
    v = [by_slot(vel_ref, k) for k in range(3)]
    w = [by_slot(spin_ref, k) for k in range(3)]
    zero = jnp.zeros((1, 128), F32)

    def four(*terms):
        out = zero
        for q, row in enumerate(terms):
            out = jnp.where(channel == q, row, out)
        return out

    constants = jnp.concatenate(
        [
            four(v[0], zero, -w[2], w[1]),
            four(v[1], w[2], zero, -w[0]),
            four(v[2], -w[1], w[0], zero),
            four(zero + 1.0, zero, zero, zero),
            by_slot(centre_ref, 2).astype(F32) + (lane % 16 - RADIUS).astype(F32),
            zero,
            zero,
            zero,
        ],
        0,
    )

    def put_beads(ref, sx, sy):
        ref[0:8] = constants
        x0, nx, _ = bead_span_x(sx, wx)
        y0, ny, _ = bead_span_y(sy, wy)
        for x in range(nx):
            start = (x0 + x) * tall + y0
            ref[8 + x * ny : 8 + (x + 1) * ny] = field[start : start + ny]

    for ref, (sx, sy) in zip(eight(bxs, bys, bcs), DIRS):
        put_beads(ref, sx, sy)
    put_beads(own, 0, 0)

    load.wait()

    def drift_plane(x, carry):
        pops = [ext[i, 1 + x, inner] for i in range(19)]
        inv = 1.0 / total_of(pops)
        for a in range(3):
            drift_ref[a, x] = momentum(pops, a) * inv
        return carry

    lax.fori_loop(0, wx, drift_plane, 0)

    def charge_at(x, y):
        return ions_ref[0, x, y] - ions_ref[1, x, y]

    for j, (sx, _) in enumerate(X_DIRS):
        out, at, edge = xs.at[j], 0, layer(sx, 0, wx)
        parts = [ext[i, 1 + edge, inner] for i in links(0, sx)]
        parts += [ions_ref[0, edge], ions_ref[1, edge], charge_at(layer(sx, 1, wx), slice(None))]
        parts += [phi_ref[layer(sx, l, wx)] for l in range(3)] + [drift_ref[0, edge]]
        for row in parts:
            out[at : at + wy] = row
            at += wy
    for j, (_, sy) in enumerate(Y_DIRS):
        out, at, edge = ys.at[j], 0, layer(sy, 0, wy)
        parts = [ext[i, 1 : 1 + wx, YO + edge] for i in links(1, sy)]
        parts += [ions_ref[0, :, edge], ions_ref[1, :, edge]]
        parts += [charge_at(slice(None), layer(sy, 1, wy))]
        parts += [phi_ref[:, layer(sy, l, wy)] for l in range(3)] + [drift_ref[1, :, edge]]
        for row in parts:
            out[at : at + wx] = row
            at += wx
    for j, (sx, sy) in enumerate(C_DIRS):
        out = cs.at[j]
        ex, ey = layer(sx, 0, wx), layer(sy, 0, wy)
        parts = [
            ext[corner_link(sx, sy), 1 + ex, YO + ey],
            charge_at(ex, ey),
            phi_ref[ex, ey],
            phi_ref[layer(sx, 1, wx), ey],
            phi_ref[ex, layer(sy, 1, wy)],
        ]
        for at, row in enumerate(parts):
            out[at] = row
        out[5:8] = jnp.zeros((3, depth), F32)
    pl.semaphore_wait(barrier, len(DIRS))
    halos = send_all(
        shape, eight(xs, ys, cs), eight(rx, ry, rc), send.at[0], recv.at[0], 1
    )

    spheres = send_all(
        shape, eight(bxs, bys, bcs), eight(bxr, byr, bcr), send.at[1], recv.at[1], 1
    )

    spread_vel = [pick(vel_ref, k) for k in range(3)]
    spin = [pick(spin_ref, k) for k in range(3)]
    cross = lambda p, q: [p[1] * q[2] - p[2] * q[1], p[2] * q[0] - p[0] * q[2], p[0] * q[1] - p[1] * q[0]]
    turn = cross(spin, lever)
    push = [weight * (spread_vel[k] + turn[k]) for k in range(3)]
    twist = cross(lever, push)
    known = [jnp.sum(t, axis=1, keepdims=True) for t in push + twist]

    for s in range(2):
        eion[s, 1 : 1 + wx, inner] = ions_ref[s]
    echarge[XO : XO + wx, inner] = ions_ref[0] - ions_ref[1]
    ephi[XO : XO + wx, inner] = phi_ref[...]
    for a in range(2):
        edrift[a, 1 : 1 + wx, inner] = drift_ref[a]
    held[...] = jnp.zeros_like(held)
    for copy in halos:
        copy.wait()
    for j, (sx, _) in enumerate(X_DIRS):
        src, at, edge = rx.at[j], 0, 1 + halo(sx, 0, wx)
        for i in links(0, sx):
            ext[i, edge, inner] = src[at : at + wy]
            at += wy
        for s in range(2):
            eion[s, edge, inner] = src[at : at + wy]
            at += wy
        echarge[XO + halo(sx, 0, wx), inner] = eion[0, edge, inner] - eion[1, edge, inner]
        echarge[XO + halo(sx, 1, wx), inner] = src[at : at + wy]
        at += wy
        for l in range(3):
            ephi[XO + halo(sx, l, wx), inner] = src[at : at + wy]
            at += wy
        edrift[0, edge, inner] = src[at : at + wy]
    for j, (_, sy) in enumerate(Y_DIRS):
        src, at, edge = ry.at[j], 0, YO + halo(sy, 0, wy)
        for i in links(1, sy):
            ext[i, 1 : 1 + wx, edge] = src[at : at + wx]
            at += wx
        ion0, ion1 = src[at : at + wx], src[at + wx : at + 2 * wx]
        eion[0, 1 : 1 + wx, edge] = ion0
        eion[1, 1 : 1 + wx, edge] = ion1
        at += 2 * wx
        echarge[XO : XO + wx, edge] = ion0 - ion1
        echarge[XO : XO + wx, YO + halo(sy, 1, wy)] = src[at : at + wx]
        at += wx
        for l in range(3):
            ephi[XO : XO + wx, YO + halo(sy, l, wy)] = src[at : at + wx]
            at += wx
        edrift[1, 1 : 1 + wx, edge] = src[at : at + wx]
    for j, (sx, sy) in enumerate(C_DIRS):
        src = rc.at[j]
        hx, hy = halo(sx, 0, wx), YO + halo(sy, 0, wy)
        ext[corner_link(sx, sy), 1 + hx, hy] = src[0]
        echarge[XO + hx, hy] = src[1]
        ephi[XO + hx, hy] = src[2]
        ephi[XO + halo(sx, 1, wx), hy] = src[3]
        ephi[XO + hx, YO + halo(sy, 1, wy)] = src[4]

    def velocity_plane(x, carry):
        read = []
        for i in range(19):
            sx, sy, sz = (int(c) for c in LATTICE[i])
            v = ext[i, 1 + x - sx, YO - sy : YO - sy + wy]
            read.append(v if sz == 0 else pltpu.roll(v, sz % depth, 1))
            streamed[i, x] = read[i]
        inverse = 1.0 / total_of(read)
        dens[x] = inverse
        for a in range(3):
            vels[a, x] = momentum(read, a) * inverse
        return carry

    lax.fori_loop(0, wx, velocity_plane, 0)

    for copy in spheres:
        copy.wait()
    save = pltpu.make_async_copy(streamed, read_out, local_sem.at[1])
    save.start()
    for n, (ref, (sx, sy)) in enumerate(zip([own] + eight(bxr, byr, bcr), [(0, 0)] + DIRS)):
        _, nx, tx = bead_span_x(sx, wx)
        _, ny, ty = bead_span_y(sy, wy)
        marks[n] = ref[0:8]
        for x in range(nx):
            held[n, tx + x, ty : ty + ny] = ref[8 + x * ny : 8 + (x + 1) * ny]
    reach = []
    for n in range(9):
        z = marks[n, 4:5].astype(jnp.int32)
        level = lax.broadcasted_iota(jnp.int32, (depth, 128), 0)
        reach.append(jnp.where(level == z, 1.0, 0.0).astype(BF16))

    parts = split3(vels[...].reshape(3 * rows, depth))
    def partial_sums(n):
        sampled = total_of(
            [lax.dot_general(p, reach[n], (((1,), (0,)), ((), ())), preferred_element_type=F32)
             for p in parts]
        )
        block = held[n].reshape(rows, 128)
        for k in range(3):
            part[n, k : k + 1] = jnp.sum(
                block * sampled[k * rows : (k + 1) * rows], axis=0, keepdims=True
            )
        part[n, 3:8] = jnp.zeros((5, 128), F32)

    for n in range(1, 9):
        partial_sums(n)
    backs = send_all(
        shape, [part.at[d + 1] for d in range(8)], [got.at[d] for d in range(8)],
        send.at[2], recv.at[2], -1,
    )
    partial_sums(0)

    def up(v):
        return jnp.where(lanes == depth - 1, 0.0, pltpu.roll(v, depth - 1, v.ndim - 1))

    def down(v):
        return jnp.where(lanes == 0, 0.0, pltpu.roll(v, 1, v.ndim - 1))

    def sweep(old, new, rim):
        lo, n = YO - rim, wy + 2 * rim

        def plane(t, carry):
            x = XO - rim + t
            mid = old[x, lo : lo + n]
            around = old[x + 1, lo : lo + n] + old[x - 1, lo : lo + n]
            around = around + (old[x, lo + 1 : lo + n + 1] + old[x, lo - 1 : lo + n - 1])
            around = around + (up(mid) + down(mid))
            new[x, lo : lo + n] = (around + kappa_charge * echarge[x, lo : lo + n]) / 6.0
            return carry

        lax.fori_loop(0, wx + 2 * rim, plane, 0)

    sweep(ephi, ephi1, 2)
    sweep(ephi1, ephi2, 1)

    def ion_plane(x, carry):
        flags = flags_ref[x]
        bit = lambda b: ((flags >> b) & 1).astype(F32)
        opened = [bit(b) for b in range(6)]
        phi = ephi2[XO + x, inner]
        phi_out[x] = phi
        phi_low = [ephi2[XO + x - 1, inner], ephi2[XO + x, YO - 1 : YO - 1 + wy]]
        phi_high = [ephi2[XO + x + 1, inner], ephi2[XO + x, YO + 1 : YO + 1 + wy]]
        phi_z_low, phi_z_high = pltpu.roll(phi, 1, 1), pltpu.roll(phi, depth - 1, 1)
        drift = [drift_ref[a, x] for a in range(3)]
        drift_low = [edrift[0, x, inner], edrift[1, 1 + x, YO - 1 : YO - 1 + wy]]
        drift_high = [edrift[0, x + 2, inner], edrift[1, 1 + x, YO + 1 : YO + 1 + wy]]
        drift_z_low = pltpu.roll(drift[2], 1, 1)

        def flux(lo_ion, hi_ion, lo_phi, hi_phi, lo_drift, hi_drift, gate, s):
            middle = 0.5 * (lo_ion + hi_ion)
            diffusive = -diffusion[s] * (
                (hi_ion - lo_ion) + valence[s] * middle * (hi_phi - lo_phi)
            )
            return gate * (diffusive + 0.5 * (lo_drift + hi_drift) * middle)

        both = []
        for s in range(2):
            ion = eion[s, 1 + x, inner]
            both.append(ion)
            ion_low = [eion[s, x, inner], eion[s, 1 + x, YO - 1 : YO - 1 + wy]]
            ion_high = [eion[s, x + 2, inner], eion[s, 1 + x, YO + 1 : YO + 1 + wy]]
            divergence = 0.0
            for a in range(2):
                entering = flux(
                    ion_low[a], ion, phi_low[a], phi, drift_low[a], drift[a], opened[2 * a], s
                )
                leaving = flux(
                    ion, ion_high[a], phi, phi_high[a], drift[a], drift_high[a], opened[2 * a + 1], s
                )
                divergence = divergence + (leaving - entering)
            entering = flux(
                pltpu.roll(ion, 1, 1), ion, phi_z_low, phi, drift_z_low, drift[2], opened[4], s
            )
            divergence = divergence + (pltpu.roll(entering, depth - 1, 1) - entering)
            ions_out[s, x] = ion - divergence
        charge = both[0] - both[1]

        field_x = (phi_low[0] - phi_high[0]) * 0.5
        field_y = (phi_low[1] - phi_high[1]) * 0.5
        field_z = (
            jnp.where(lanes == 0, 0.0, phi_z_low) - jnp.where(lanes == depth - 1, 0.0, phi_z_high)
        ) * 0.5
        scale = tau_relax * charge * dens[x]
        for a, e in enumerate((field_x, field_y, field_z)):
            shifted_out[a, x] = vels[a, x] + scale * e
        return carry

    lax.fori_loop(0, wx, ion_plane, 0)

    for n in range(9):
        block = held[n].reshape(rows, 128)
        for k in range(4):
            for p, piece in enumerate(split3(block * marks[n, k : k + 1])):
                bead_rows[p, k * rows : (k + 1) * rows, n * 128 : (n + 1) * 128] = piece
    everywhere = jnp.concatenate(reach, 1)
    spread = total_of([dot_t(bead_rows[p], everywhere) for p in range(3)])
    pushes[...] = spread.reshape(4, wx, wy, depth)
    scale = (tau_relax * friction) * dens[...]
    for a in range(3):
        shifted_out[a] += scale * (pushes[a] - pushes[3] * vels[a])

    save.wait()
    for copy in backs:
        copy.wait()
    whole = total_of([part[0]] + [got[d] for d in range(8)])
    group = lax.broadcasted_iota(jnp.int32, (8, 128), 1) // 16
    for s in range(2):
        m = [
            jnp.sum(jnp.where(group == 4 * s + q, whole, 0.0), axis=1, keepdims=True)
            for q in range(4)
        ]
        mean = [m[0][k : k + 1] for k in range(3)]
        lev = [[m[1 + a][k : k + 1] for k in range(3)] for a in range(3)]
        turned = [lev[1][2] - lev[2][1], lev[2][0] - lev[0][2], lev[0][1] - lev[1][0]]
        for k, t in enumerate(mean + turned):
            kick_ref[s : s + 1, k : k + 1] = (known[k][s : s + 1] - t) * (-friction / nb)


def second_kernel(
    read_ref, shifted_ref, flags_ref, ions_ref, phi_ref, kick_ref,
    pops_out, ions_out, phi_out, kick_out,
):
    kick_out[...] = kick_ref[...]

    def collide_plane(x, carry):
        phi_out[x] = phi_ref[x]
        for s in range(2):
            ions_out[s, x] = ions_ref[s, x]
        solid = ((flags_ref[x] >> 6) & 1) == 1
        read = [read_ref[i, x] for i in range(19)]
        density = total_of(read)
        shifted = [shifted_ref[a, x] for a in range(3)]
        base = 1.0 - 1.5 * (
            shifted[0] * shifted[0] + shifted[1] * shifted[1] + shifted[2] * shifted[2]
        )
        scaled = [w * density * (1.0 / tau_relax) for w in (1.0 / 3.0, 1.0 / 18.0, 1.0 / 36.0)]
        keep = 1.0 - 1.0 / tau_relax
        pops_out[0, x] = jnp.where(solid, read[0], keep * read[0] + scaled[0] * base)
        for i in range(1, 19, 2):
            along = 0.0
            for a in range(3):
                if LATTICE[i][a] != 0:
                    along = along + float(LATTICE[i][a]) * shifted[a]
            even = base + 4.5 * along * along
            odd = 3.0 * along
            scale = scaled[1] if i < 7 else scaled[2]
            pops_out[i, x] = jnp.where(
                solid, read[i + 1], keep * read[i] + scale * (even + odd)
            )
            pops_out[i + 1, x] = jnp.where(
                solid, read[i], keep * read[i + 1] + scale * (even - odd)
            )
        return carry

    lax.fori_loop(0, phi_ref.shape[0], collide_plane, 0)


def local(
    shape, populations, ion_density, potential, node_flags, colloid_count, colloid_centre,
    colloid_velocity, colloid_spin, bead_cell, bead_frac, bead_weight,
):
    wx, wy, depth = potential.shape
    kp = -(-bead_cell.shape[3] // 256) * 256
    vmem = pl.BlockSpec(memory_space=pltpu.VMEM)
    smem = pl.BlockSpec(memory_space=pltpu.SMEM)
    hbm = pl.BlockSpec(memory_space=pl.ANY)
    array = lambda *dims: jax.ShapeDtypeStruct(dims, F32)
    mem = lambda *dims: pltpu.VMEM(dims, F32)
    by_slot = lambda a: jnp.transpose(a, (1, 2, 3, 0)).reshape(a.shape[3], a.shape[0])
    tall, wide, far = wy + 2 * YO, wx + 2, wx + 2 * XO
    slabs = [mem(2, 12 * wy, depth), mem(2, 12 * wx, depth), mem(4, 8, depth)]
    balls = [mem(2, 8 + RADIUS * wy, 128), mem(2, 8 + wx * 8, 128), mem(4, 8 + RADIUS * 8, 128)]
    read, shifted, ions, phi, kick = pl.pallas_call(
        functools.partial(first_kernel, shape),
        out_shape=[
            array(*populations.shape), array(3, wx, wy, depth), array(*ion_density.shape),
            array(*potential.shape), array(2, 6),
        ],
        in_specs=[smem] * 4 + [vmem] * 3 + [hbm] + [vmem] * 3,
        out_specs=[hbm] + [vmem] * 4,
        scratch_shapes=slabs + slabs + balls + balls + [
            mem(8 + wx * wy, 128),
            mem(3, wx, wy, depth),
            mem(5, 2, kp),
            mem(6, 2, kp),
            mem(SIDE + 2 * (wx - 1), tall, 192),
            mem((wx + 2 * RADIUS) * tall, 128),
            mem(19, wide, tall, depth),
            mem(2, wide, tall, depth),
            mem(far, tall, depth),
            mem(2, wide, tall, depth),
            mem(far, tall, depth),
            mem(far, tall, depth),
            mem(far, tall, depth),
            mem(9, wx, wy, 128),
            mem(9, 8, 128),
            pltpu.VMEM((3, 4 * wx * wy, 9 * 128), BF16),
            mem(4, wx, wy, depth),
            mem(3, wx, wy, depth),
            mem(wx, wy, depth),
            mem(9, 8, 128),
            mem(8, 8, 128),
            mem(*populations.shape),
            pltpu.SemaphoreType.DMA((3, 8)),
            pltpu.SemaphoreType.DMA((3, 8)),
            pltpu.SemaphoreType.DMA((2,)),
        ],
        compiler_params=pltpu.CompilerParams(collective_id=0, has_side_effects=True),
    )(
        colloid_count, by_slot(colloid_centre), by_slot(colloid_velocity), by_slot(colloid_spin),
        bead_cell, bead_frac, bead_weight, populations, ion_density, potential, node_flags,
    )
    pops_next, ions_next, phi_next, kick = pl.pallas_call(
        second_kernel,
        out_shape=[
            array(*populations.shape), array(*ion_density.shape), array(*potential.shape),
            array(2, 6),
        ],
        in_specs=[vmem] * 6,
        out_specs=[vmem] * 4,
    )(read, shifted, node_flags, ions, phi, kick)
    return pops_next, ions_next, phi_next, jnp.transpose(kick.reshape(1, 1, 2, 6), (3, 0, 1, 2))


def solution(mesh):
    in_specs = (
        P(None, "gx", "gy", None),
        P(None, "gx", "gy", None),
        P("gx", "gy", None),
        P("gx", "gy", None),
        P("gx", "gy"),
        P(None, "gx", "gy", None),
        P(None, "gx", "gy", None),
        P(None, "gx", "gy", None),
        P("gx", "gy", None, None),
        P(None, "gx", "gy", None, None),
        P("gx", "gy", None, None),
    )
    out_specs = (
        P(None, "gx", "gy", None),
        P(None, "gx", "gy", None),
        P("gx", "gy", None),
        P(None, "gx", "gy", None),
    )
    shape = (mesh.shape["gx"], mesh.shape["gy"])
    return jax.shard_map(
        functools.partial(local, shape), mesh=mesh, in_specs=in_specs, out_specs=out_specs,
        check_vma=False,
    )
```
